128 devices in a mesh: tr: 8 (over z, core), tc: 16 (over y, x).
Axes of the slice: x: 4, y: 4, z: 4, core: 2. Of those that a mesh axis runs over, the one named last changes fastest.
Arguments:
- object_init: float32 [2, 4096, 8192], P(None, 'tr', 'tc'), may hold values from -6 to 6
- probe_init: float32 [2, 512, 512], replicated, may hold values from -6 to 6
- moduli: float32 [256, 512, 512], P(('tr', 'tc')), may hold values from 0.1 to 3
- corners: int32 [256, 2], P(('tr', 'tc')), may hold values from 0 to 7680, as said below
- live: int32 [256], P(('tr', 'tc')), may hold values from 0 to 1, as said below
Outputs:
- object_out: float32 [2, 4096, 8192], P(None, 'tr', 'tc')
- probe_out: float32 [2, 512, 512], replicated
The draws below stay inside these ranges and needn't reach their ends.
Inputs may be any that keep to these rules, and one draw needn't show every extreme that they name: `corners`: views are held in scan order, 2 slots to a device in the device order of tr+tc; a view's corner lies in the object tile of the device that holds it, and its 512 x 512 patch lies inside the object. Every device holds at least one live view.
All inputs are finite; a program needn't handle non-finite values.
Results may differ from the reference program's by a relative error of at most 0.0003.
Values sent between devices are 32-bit elements; how exact they have to be, the bound alone decides.
No kernel may reach another device: no remote copies, remote signals or barrier semaphores. Data moves between devices by JAX's collectives and lax.ppermute only.
A program may use at most 128 MiB of HBM per device.

```python
import math
import jax
import jax.numpy as jnp
from jax import lax

W = 512
TILE_R = 512
TILE_C = 512
SLOT_DEV = 2
ITERS = 2
NR = 4096
NC = 8192
VIEWS = 256


def reach_choice(key):
    tiles_down = NR // TILE_R
    tiles_across = NC // TILE_C
    key_row, key_col, key_slot = jax.random.split(jax.random.fold_in(key, 31), 3)
    pick_row = jax.random.randint(key_row, (), 0, tiles_down - 1)
    pick_col = jax.random.randint(key_col, (), 0, tiles_across - 1)
    pick_slot = jax.random.randint(key_slot, (), 0, SLOT_DEV)
    return ((pick_row * tiles_across + pick_col) * SLOT_DEV + pick_slot).astype(jnp.int32)


def draw_corners(key, part):
    tiles_down = NR // TILE_R
    tiles_across = NC // TILE_C
    view_index = jnp.arange(VIEWS, dtype=jnp.int32)
    device_index = view_index // SLOT_DEV
    row_dev = device_index // tiles_across
    col_dev = device_index % tiles_across
    row_limit = jnp.where(row_dev == tiles_down - 1, TILE_R - W + 1, TILE_R).astype(jnp.int32)
    col_limit = jnp.where(col_dev == tiles_across - 1, TILE_C - W + 1, TILE_C).astype(jnp.int32)
    key_rows, key_cols = jax.random.split(jax.random.fold_in(key, 11))
    row_offset = jax.random.randint(key_rows, (VIEWS,), 0, row_limit)
    col_offset = jax.random.randint(key_cols, (VIEWS,), 0, col_limit)
    reach_view = reach_choice(key)
    row_offset = jnp.where(view_index == reach_view, TILE_R - 1, row_offset)
    col_offset = jnp.where(view_index == reach_view, TILE_C - 1, col_offset)
    final_view = (VIEWS // SLOT_DEV - 1) * SLOT_DEV
    row_offset = jnp.where(view_index == final_view, TILE_R - W, row_offset)
    col_offset = jnp.where(view_index == final_view, TILE_C - W, col_offset)
    return jnp.stack([row_dev * TILE_R + row_offset, col_dev * TILE_C + col_offset], 1).astype(jnp.int32)


def draw_live(key, part):
    key_bits, key_forced = jax.random.split(jax.random.fold_in(key, 23))
    random_bits = jax.random.randint(key_bits, (VIEWS,), 0, 2)
    forced_slot = jax.random.randint(key_forced, (VIEWS // SLOT_DEV,), 0, SLOT_DEV)
    view_index = jnp.arange(VIEWS, dtype=jnp.int32)
    slot_index = view_index % SLOT_DEV
    forced = (slot_index == jnp.repeat(forced_slot, SLOT_DEV)).astype(jnp.int32)
    reaching = (view_index == reach_choice(key)).astype(jnp.int32)
    return jnp.maximum(jnp.maximum(random_bits, forced), reaching).astype(jnp.int32)


def steps_of(rng, shape, shards, least, largest):
    def one(position, blocks):
        steps = jax.random.uniform(jax.random.fold_in(jax.random.fold_in(rng, 6), position), (blocks,), jnp.float32, least / len(shards), largest / len(shards))
        return jnp.repeat(jnp.exp(steps), shape[position] // blocks).reshape((-1,) + (1,) * (len(shape) - position - 1))

    factor_of = one(*shards[0])
    for cut in shards[1:]:
        factor_of = factor_of * one(*cut)
    return factor_of


def scatter_about(stream_key, shape, spread, most, pieces=(), held_as=jnp.bfloat16):
    factor_of = steps_of(stream_key, shape, pieces, -0.22, 0.18) if pieces else 1.0
    array = jax.random.normal(stream_key, shape, jnp.float32) * spread * factor_of
    return jnp.minimum(jnp.maximum(array, -most), most).astype(held_as)


def setup_inputs(seed: int = 0) -> dict:
    streams_of = jax.random.split(jax.random.key(seed), 6)
    object_init = scatter_about(streams_of[0], (2, NR, NC), 1.0, 6.0, ((1, 8), (2, 16)), jnp.float32)
    probe_init = scatter_about(streams_of[1], (2, W, W), 1.0, 6.0, (), jnp.float32)
    moduli = jnp.clip(jnp.exp(math.log(3.0) - 3.4011974 * jax.random.uniform(streams_of[2], (VIEWS, W, W), jnp.float32) ** steps_of(streams_of[2], (VIEWS, W, W), ((0, 128),), -0.2, 0.2)), 0.1, 3.0)
    corners = draw_corners(jax.random.fold_in(streams_of[5], 71), 0)
    live = draw_live(jax.random.fold_in(streams_of[5], 71), 0)
    return dict(object_init=object_init, probe_init=probe_init, moduli=moduli, corners=corners, live=live)


HIGH = lax.Precision.HIGHEST
FLOOR = 0.1
EPS = 1e-06
ALPHA_STEP = 1.0
BETA_STEP = 1.0

def dft_tables(side):
    index = jnp.arange(side, dtype=jnp.int32)
    phase = index[:, None] * index[None, :] % side
    angle = phase.astype(jnp.float32) * (2.0 * math.pi / side)
    root = 1.0 / math.sqrt(side)
    return (jnp.cos(angle) * root, jnp.sin(angle) * root)

def apply_left(mat_re, mat_im, arr_re, arr_im):
    prod_one = jnp.dot(mat_re, arr_re, precision=HIGH, preferred_element_type=jnp.float32)
    prod_two = jnp.dot(mat_im, arr_im, precision=HIGH, preferred_element_type=jnp.float32)
    prod_three = jnp.dot(mat_re + mat_im, arr_re + arr_im, precision=HIGH, preferred_element_type=jnp.float32)
    return (prod_one - prod_two, prod_three - prod_one - prod_two)

def apply_right(arr_re, arr_im, mat_re, mat_im):
    prod_one = jnp.dot(arr_re, mat_re, precision=HIGH, preferred_element_type=jnp.float32)
    prod_two = jnp.dot(arr_im, mat_im, precision=HIGH, preferred_element_type=jnp.float32)
    prod_three = jnp.dot(arr_re + arr_im, mat_re + mat_im, precision=HIGH, preferred_element_type=jnp.float32)
    return (prod_one - prod_two, prod_three - prod_one - prod_two)

def transform(arr_re, arr_im, mat_re, mat_im):
    mid_re, mid_im = apply_left(mat_re, mat_im, arr_re, arr_im)
    return apply_right(mid_re, mid_im, mat_re, mat_im)

def view_update(probe_now, patch, measured, cosines, sines):
    wave_re = probe_now[0] * patch[0] - probe_now[1] * patch[1]
    wave_im = probe_now[0] * patch[1] + probe_now[1] * patch[0]
    far_re, far_im = transform(wave_re, wave_im, cosines, -sines)
    amplitude = jnp.sqrt(far_re * far_re + far_im * far_im)
    factor = measured / jnp.maximum(amplitude, FLOOR) - 1.0
    chi_re, chi_im = transform(far_re * factor, far_im * factor, cosines, sines)
    object_grad = jnp.stack([probe_now[0] * chi_re + probe_now[1] * chi_im, probe_now[0] * chi_im - probe_now[1] * chi_re])
    probe_grad = jnp.stack([patch[0] * chi_re + patch[1] * chi_im, patch[0] * chi_im - patch[1] * chi_re])
    return (object_grad, probe_grad)

def reference(object_init, probe_init, moduli, corners, live):
    cosines, sines = dft_tables(W)
    object_now = object_init
    probe_now = probe_init
    for iteration in range(ITERS):

        def visit(carry, inputs):
            object_grad, probe_grad = carry
            corner, alive, measured = inputs
            corner_at = (jnp.zeros((), jnp.int32), corner[0].astype(jnp.int32), corner[1].astype(jnp.int32))
            patch = lax.dynamic_slice(object_now, corner_at, (2, W, W))
            view_object, view_probe = view_update(probe_now, patch, measured, cosines, sines)
            weight = alive.astype(jnp.float32)
            current = lax.dynamic_slice(object_grad, corner_at, (2, W, W))
            object_grad = lax.dynamic_update_slice(object_grad, current + weight * view_object, corner_at)
            return ((object_grad, probe_grad + weight * view_probe), None)
        start_pair = (jnp.zeros_like(object_now), jnp.zeros_like(probe_now))
        totals, unused = lax.scan(visit, start_pair, (corners, live, moduli))
        object_grad, probe_grad = totals
        view_count = jnp.sum(live).astype(jnp.float32)
        probe_power = jnp.max(probe_now[0] * probe_now[0] + probe_now[1] * probe_now[1]) + EPS
        object_now = object_now + ALPHA_STEP * object_grad / probe_power
        probe_now = probe_now + BETA_STEP * probe_grad / view_count
    return (object_now, probe_now)
```

```python
import math

import jax
import jax.numpy as jnp
import numpy as np
from jax import lax
from jax.experimental import pallas as pl
from jax.experimental.pallas import tpu as pltpu
from jax.sharding import PartitionSpec as P


ITERS = 2
W = 512
Q = 128
CHUNKS = 2
FLOOR = 0.1
EPS = 1e-06
F32 = jnp.float32
BF = jnp.bfloat16
RB = 32
R4 = 64
AXES = ("tr", "tc")
SIZES = {"c": 2, "x": 4, "y": 4, "z": 4}


def shifted(x, axis, by):
    peers = lax.axis_size(axis)
    pairs = [(i, i + by) for i in range(peers) if 0 <= i + by < peers]
    return lax.ppermute(x, axis, pairs)


def turned(x, axis, by):
    pairs = []
    for tr in range(8):
        for tc in range(16):
            at = {"x": tc % 4, "y": tc // 4, "z": tr // 2, "c": tr % 2}
            to = dict(at)
            to[axis] = (at[axis] + by) % SIZES[axis]
            pairs.append((tr * 16 + tc, (to["z"] * 2 + to["c"]) * 16 + to["y"] * 4 + to["x"]))
    return lax.ppermute(x, AXES, pairs)


def scatter_stage(v, tag, axis, at):
    size = SIZES[axis]
    rows = v.shape[0] // size
    own = lax.dynamic_slice_in_dim(v, at[axis] * rows, rows, 0)
    whole = jnp.concatenate([own, tag], 0)
    for by in range(1, size):
        piece = lax.dynamic_slice_in_dim(v, ((at[axis] + by) % size) * rows, rows, 0)
        whole = whole + turned(jnp.concatenate([piece, tag], 0), axis, by)
    return whole[:rows], whole[rows:]


def exchange_stage(v, tag, axis, at):
    size = SIZES[axis]
    own = jnp.concatenate([v, tag], 0)
    got = [own] + [turned(own, axis, by) for by in range(1, size)]
    whole = None
    for k in range(size):
        term = got[0]
        for by in range(1, size):
            term = jnp.where((at[axis] - by) % size == k, got[by], term)
        whole = term if whole is None else whole + term
    return whole[: v.shape[0]], whole[v.shape[0] :]


def gather_stage(v, axis, at):
    size = SIZES[axis]
    rows = v.shape[0]
    out = jnp.zeros((size * rows,) + v.shape[1:], v.dtype)
    out = lax.dynamic_update_slice_in_dim(out, v, at[axis] * rows, 0)
    for by in range(1, size):
        got = turned(v, axis, by)
        out = lax.dynamic_update_slice_in_dim(out, got, ((at[axis] - by) % size) * rows, 0)
    return out


def next_probe(probe_now, grad, weight_sum, at):
    flat = grad.reshape(2 * W, W)
    tag = jnp.full((8, W), 1.0, F32) * weight_sum
    start = jnp.zeros((), jnp.int32)
    rows = 2 * W
    for axis in ("c", "x", "y"):
        flat, tag = scatter_stage(flat, tag, axis, at)
        rows //= SIZES[axis]
        start = start + at[axis] * rows
    flat, tag = exchange_stage(flat, tag, "z", at)
    own = lax.dynamic_slice_in_dim(probe_now.reshape(2 * W, W), start, rows, 0)
    own = own + flat / tag[0, 0]
    for axis in ("y", "x", "c"):
        own = gather_stage(own, axis, at)
    return own.reshape(2, W, W)


def tables():
    k = np.arange(Q)[:, None]
    n = np.arange(Q)[None, :]
    parts = []
    for q in range(4):
        angle = 2 * np.pi * (((4 * k + q) * n) % W) / W
        c, s = np.cos(angle) / math.sqrt(W), np.sin(angle) / math.sqrt(W)
        parts.append(np.block([[c, s], [-s, c]]))
    whole = np.stack(parts).astype(np.float32)
    high = whole.astype(jnp.bfloat16)
    low = (whole - high.astype(np.float32)).astype(jnp.bfloat16)
    turn = lambda a: np.ascontiguousarray(np.swapaxes(a, 1, 2))
    return high, low, turn(high), turn(low)


def split(x):
    high = x.astype(BF)
    return high, (x - high.astype(F32)).astype(BF)


def sums(x):
    return x[0] + x[2], x[0] - x[2], x[1] + x[3], x[1] - x[3]


def forward4(re, im):
    s0r, d0r, s1r, d1r = sums(re)
    s0i, d0i, s1i, d1i = sums(im)
    return [
        (s0r + s1r, s0i + s1i),
        (d0r + d1i, d0i - d1r),
        (s0r - s1r, s0i - s1i),
        (d0r - d1i, d0i + d1r),
    ]


def inverse4(re, im):
    s0r, d0r, s1r, d1r = sums(re)
    s0i, d0i, s1i, d1i = sums(im)
    return [
        (s0r + s1r, s0i + s1i),
        (d0r - d1i, d0i + d1r),
        (s0r - s1r, s0i - s1i),
        (d0r + d1i, d0i - d1r),
    ]


def dot(a, b):
    return jnp.dot(a, b, preferred_element_type=F32)


def at_row(start, count):
    return pl.ds(pl.multiple_of(start, 8), count)


def at_row32(start, count):
    return pl.ds(pl.multiple_of(start, 32), count)


def order_kernel(m_ref, o_ref, held):
    row = lax.broadcasted_iota(jnp.int32, (W, W), 0)
    col = lax.broadcasted_iota(jnp.int32, (W, W), 1)
    pick = jnp.where(row == 4 * (col % Q) + col // Q, 1.0, 0.0).astype(BF)
    for v in range(2):
        for b in range(4):
            held[b * W : (b + 1) * W, :] = m_ref[v, :, b * Q : (b + 1) * Q]
        for q in range(4):
            x = jnp.concatenate([held[pl.ds(b * W + q, Q, stride=4), :] for b in range(4)], 1)
            high = x.astype(BF)
            rest = x - high.astype(F32)
            mid, low = split(rest)
            o_ref[v, q * Q : (q + 1) * Q, :] = (dot(high, pick) + dot(mid, pick)) + dot(low, pick)


def ordered(m):
    vm = pl.BlockSpec(memory_space=pltpu.VMEM)
    return pl.pallas_call(
        order_kernel,
        out_shape=jax.ShapeDtypeStruct((2, W, W), F32),
        in_specs=[vm],
        out_specs=vm,
        scratch_shapes=[pltpu.VMEM((4 * W, Q), F32)],
        compiler_params=pltpu.CompilerParams(vmem_limit_bytes=32 * 1024 * 1024),
        cost_estimate=pl.CostEstimate(flops=6 * W**3 * 2, bytes_accessed=16 * W * W, transcendentals=0),
        name="order",
    )(m)


def views_kernel(sc, wt, *refs):
    n = CHUNKS
    t_refs, r_refs, b_refs, d_refs = (refs[k * n : (k + 1) * n] for k in range(4))
    refs = refs[4 * n :]
    p_ref, m_ref, mh, ml, th, tl = refs[:6]
    refs = refs[6:]
    own_refs, gr_refs, gb_refs, gd_refs = (refs[k * n : (k + 1) * n] for k in range(4))
    pg_ref, pr, s1, xx, dd, ee, zz, pp = refs[4 * n :]
    span = W // n

    def roll_rows(t, top):
        rows, rows2 = at_row(t * RB, RB), at_row(t * RB + W, RB)
        before = at_row(jnp.where(t == 0, W - 8, t * RB - 8), 8)
        re, im = p_ref[0, rows, :], p_ref[1, rows, :]
        for k, x in ((0, re), (1, im)):
            x = jnp.concatenate([p_ref[k, before, :], x], 0)
            for v in range(2):
                y = pltpu.roll(pltpu.roll(x, sc[2 * v + 1], 1), sc[2 * v] & 7, 0)[8:]
                pr[v, k, rows, :] = y
                pr[v, k, rows2, :] = y
        return jnp.maximum(top, re * re + im * im)

    top = lax.fori_loop(0, W // RB, roll_rows, jnp.zeros((RB, W), F32))
    step = 1.0 / (jnp.max(top) + EPS)
    lanes = lax.broadcasted_iota(jnp.int32, (1, W), 1)

    def pick(v, chunk, start, count):
        row = chunk * span + start + lax.broadcasted_iota(jnp.int32, (count, 1), 0)
        below = jnp.broadcast_to(row < sc[2 * v], (count, W))
        right = jnp.broadcast_to(lanes < sc[2 * v + 1], (count, W))
        rows = at_row(start, count)
        out = []
        for k in range(2):
            upper = jnp.where(right, r_refs[chunk][k, rows, :], t_refs[chunk][k, rows, :])
            lower = jnp.where(right, d_refs[chunk][k, rows, :], b_refs[chunk][k, rows, :])
            out.append(jnp.where(below, lower, upper))
        return out[0], out[1], below, right

    def probe_rows(v, row, count):
        rows = at_row(W - (sc[2 * v] & -8) + row, count)
        return pr[v, 0, rows, :], pr[v, 1, rows, :]

    for v in range(2):

        def first(t, _):
            base = t * RB
            for p in range(4):
                chunk, start = divmod(p * Q, span)
                are, aim, _b, _r = pick(v, chunk, start + base, RB)
                pre, pim = probe_rows(v, base + p * Q, RB)
                wr, wi = pre * are - pim * aim, pre * aim + pim * are
                cols = [slice(q * Q, (q + 1) * Q) for q in range(4)]
                o = slice(p * RB, (p + 1) * RB)
                for q, (br, bi) in enumerate(forward4([wr[:, c] for c in cols], [wi[:, c] for c in cols])):
                    s1[q, o, 0:128], s1[q, o, 256:384] = split(br)
                    s1[q, o, 128:256], s1[q, o, 384:512] = split(bi)
            for q in range(4):
                high, low = s1[q, :, 0:256], s1[q, :, 256:512]
                a = dot(high, th[q]) + dot(low, th[q]) + dot(high, tl[q])
                re = [a[p * RB : (p + 1) * RB, 0:Q] for p in range(4)]
                im = [a[p * RB : (p + 1) * RB, Q:] for p in range(4)]
                c = slice(q * Q, (q + 1) * Q)
                for u, (br, bi) in enumerate(forward4(re, im)):
                    xx[u, at_row32(base, RB), c], xx[u, at_row32(base + 256, RB), c] = split(br)
                    xx[u, at_row32(base + 128, RB), c], xx[u, at_row32(base + 384, RB), c] = split(bi)
            return 0

        lax.fori_loop(0, Q // RB, first, 0)
        for half in range(2):
            cs = slice(half * 256, (half + 1) * 256)

            def middle(u, _):
                high, low = xx[u, 0:256, cs], xx[u, 256:512, cs]
                far = dot(mh[u], high) + dot(mh[u], low) + dot(ml[u], high)
                re, im = far[0:Q], far[Q:]
                size = jnp.maximum(re * re + im * im, FLOOR * FLOOR)
                f = m_ref[v, at_row(u * Q, Q), cs] * lax.rsqrt(size) - 1.0
                dd[0:128, :], dd[256:384, :] = split(re * f)
                dd[128:256, :], dd[384:512, :] = split(im * f)
                high, low = dd[0:256, :], dd[256:512, :]
                ee[u] = dot(th[u], high) + dot(th[u], low) + dot(tl[u], high)
                return 0

            lax.fori_loop(0, 4, middle, 0)

            def turn(t, _):
                ro, io = at_row(t * RB, RB), at_row(t * RB + Q, RB)
                for h in range(2):
                    c = slice(h * Q, (h + 1) * Q)
                    qc = 2 * half + h
                    parts = inverse4([ee[u, ro, c] for u in range(4)], [ee[u, io, c] for u in range(4)])
                    for p, (zr, zi) in enumerate(parts):
                        o = at_row32(t * RB + p * Q, RB)
                        zz[v, qc, o, 0:128], zz[v, qc, o, 256:384] = split(zr)
                        zz[v, qc, o, 128:256], zz[v, qc, o, 384:512] = split(zi)
                return 0

            lax.fori_loop(0, Q // RB, turn, 0)

    for chunk in range(n):

        def last(t, _):
            start = t * R4
            rows = at_row(start, R4)
            all_rows = at_row32(chunk * span + start, R4)
            for v in range(2):
                e = []
                for q in range(4):
                    high, low = zz[v, q, all_rows, 0:256], zz[v, q, all_rows, 256:512]
                    e.append(dot(high, mh[q]) + dot(low, mh[q]) + dot(high, ml[q]))
                parts = inverse4([x[:, 0:Q] for x in e], [x[:, Q:] for x in e])
                cr = jnp.concatenate([x[0] for x in parts], 1) * wt[v]
                ci = jnp.concatenate([x[1] for x in parts], 1) * wt[v]
                are, aim, below, right = pick(v, chunk, start, R4)
                pre, pim = probe_rows(v, chunk * span + start, R4)
                grad = ((pre * cr + pim * ci) * step, (pre * ci - pim * cr) * step)
                pp[v, 0, all_rows, :] = pltpu.roll(are * cr + aim * ci, W - sc[2 * v + 1], 1)
                pp[v, 1, all_rows, :] = pltpu.roll(are * ci - aim * cr, W - sc[2 * v + 1], 1)
                none = jnp.zeros_like(cr)
                for k in range(2):
                    upper, lower = jnp.where(below, none, grad[k]), jnp.where(below, grad[k], none)
                    terms = (
                        (own_refs, jnp.where(right, none, upper)),
                        (gr_refs, jnp.where(right, upper, none)),
                        (gb_refs, jnp.where(right, none, lower)),
                        (gd_refs, jnp.where(right, lower, none)),
                    )
                    for which, term in terms:
                        if v == 0:
                            if which is own_refs:
                                term = term + t_refs[chunk][k, rows, :]
                            which[chunk][k, rows, :] = term
                        else:
                            which[chunk][k, rows, :] += term
            return 0

        lax.fori_loop(0, span // R4, last, 0)

    def double(t, _):
        rows, rows2 = at_row(t * RB, RB), at_row(t * RB + W, RB)
        for v in range(2):
            for k in range(2):
                x = pp[v, k, rows, :]
                pr[v, k, rows, :] = x
                pr[v, k, rows2, :] = x
        return 0

    lax.fori_loop(0, W // RB, double, 0)

    def back(t, _):
        for k in range(2):
            total = None
            for v in range(2):
                x = pr[v, k, at_row((sc[2 * v] & -8) + t * RB, RB + 8), :]
                x = pltpu.roll(x, RB + 8 - (sc[2 * v] & 7), 0)[:RB]
                total = x if total is None else total + x
            pg_ref[k, at_row(t * RB, RB), :] = total
        return 0

    lax.fori_loop(0, W // RB, back, 0)


def views(sc, wt, tiles, probe_now, moduli, tabs):
    vm, sm = pl.BlockSpec(memory_space=pltpu.VMEM), pl.BlockSpec(memory_space=pltpu.SMEM)
    part = jax.ShapeDtypeStruct((2, W // CHUNKS, W), F32)
    out = pl.pallas_call(
        views_kernel,
        out_shape=(part,) * (4 * CHUNKS) + (jax.ShapeDtypeStruct((2, W, W), F32),),
        in_specs=[sm, sm] + [vm] * (4 * CHUNKS + 6),
        out_specs=(vm,) * (4 * CHUNKS + 1),
        scratch_shapes=[
            pltpu.VMEM((2, 2, 2 * W, W), F32),
            pltpu.VMEM((4, 4 * RB, 512), BF),
            pltpu.VMEM((4, 512, W), BF),
            pltpu.VMEM((512, 256), BF),
            pltpu.VMEM((4, 256, 256), F32),
            pltpu.VMEM((2, 4, W, 512), BF),
            pltpu.VMEM((2, 2, W, W), F32),
        ],
        compiler_params=pltpu.CompilerParams(vmem_limit_bytes=58 * 1024 * 1024),
        cost_estimate=pl.CostEstimate(flops=26 * 10**9, bytes_accessed=28 * 2**20, transcendentals=2**19),
        name="views",
    )(sc, wt, *[x for tile in tiles for x in tile], probe_now, moduli, *tabs)
    return [out[k * CHUNKS : (k + 1) * CHUNKS] for k in range(4)], out[-1]


def on_device(object_init, probe_init, moduli, corners, live):
    tr, tc = lax.axis_index("tr"), lax.axis_index("tc")
    at = {"x": tc % 4, "y": tc // 4, "z": tr // 2, "c": tr % 2}
    sc = (corners - jnp.stack([tr * W, tc * W])).astype(jnp.int32).reshape(-1)
    wt = live.astype(F32)
    tabs = [jnp.asarray(a) for a in tables()]
    span = W // CHUNKS
    tile = [object_init[:, i * span : (i + 1) * span] for i in range(CHUNKS)]
    probe_now = probe_init
    measured = ordered(moduli)
    for iteration in range(ITERS):
        right = [shifted(x, "tc", -1) for x in tile]
        below = [shifted(x, "tr", -1) for x in tile]
        corner = [shifted(x, "tr", -1) for x in right]
        (own, g_right, g_below, g_corner), grad = views(
            sc, wt, (tile, right, below, corner), probe_now, measured, tabs
        )
        tile = []
        for i in range(CHUNKS):
            g = g_right[i] + shifted(g_corner[i], "tr", 1)
            tile.append(own[i] + shifted(g_below[i], "tr", 1) + shifted(g, "tc", 1))
        probe_now = next_probe(probe_now, grad, jnp.sum(wt), at)
    return jnp.concatenate(tile, 1), probe_now


def solution(mesh):
    placed = (
        P(None, "tr", "tc"),
        P(),
        P(("tr", "tc"), None, None),
        P(("tr", "tc"), None),
        P(("tr", "tc")),
    )
    return jax.shard_map(
        on_device, mesh=mesh, in_specs=placed, out_specs=(P(None, "tr", "tc"), P()), check_vma=False
    )
```

```python
import math

import jax
import jax.numpy as jnp
from jax import lax
from jax.experimental import pallas as pl
from jax.experimental.pallas import tpu as pltpu
from jax.sharding import PartitionSpec as P


ITERS = 2
W = 512
Q = 128
ROWS = 1
CHUNKS = 2 * ROWS
FLOOR = 0.1
EPS = 1e-06
F32 = jnp.float32
BF = jnp.bfloat16
RB = 32
R4 = 128
AXES = ("tr", "tc")
SIZES = {"c": 2, "x": 4, "y": 4, "z": 4}


def shifted(x, axis, by):
    peers = lax.axis_size(axis)
    pairs = [(i, i + by) for i in range(peers) if 0 <= i + by < peers]
    return lax.ppermute(x, axis, pairs)


def turned(x, axis, by):
    pairs = []
    for tr in range(8):
        for tc in range(16):
            at = {"x": tc % 4, "y": tc // 4, "z": tr // 2, "c": tr % 2}
            to = dict(at)
            to[axis] = (at[axis] + by) % SIZES[axis]
            pairs.append((tr * 16 + tc, (to["z"] * 2 + to["c"]) * 16 + to["y"] * 4 + to["x"]))
    return lax.ppermute(x, AXES, pairs)


def pieces_of(v, tag, axis, at):
    size = SIZES[axis]
    rows = v.shape[0] // size
    out = []
    for by in range(1, size):
        piece = lax.dynamic_slice_in_dim(v, ((at[axis] + by) % size) * rows, rows, 0)
        out.append(jnp.concatenate([piece, tag], 0))
    return out


def sum_up(v, tag, got, axis, at):
    rows = v.shape[0] // SIZES[axis]
    whole = lax.dynamic_slice_in_dim(v, at[axis] * rows, rows, 0)
    for x in got:
        whole, tag = whole + x[:rows], tag + x[rows:]
    return whole, tag


def sum_in_order(own, got, axis, at):
    size = SIZES[axis]
    got = [own] + got
    whole = None
    for k in range(size):
        term = got[0]
        for by in range(1, size):
            term = jnp.where((at[axis] - by) % size == k, got[by], term)
        whole = term if whole is None else whole + term
    return whole


def placed_in(v, got, axis, at):
    size, rows = SIZES[axis], v.shape[0]
    out = jnp.zeros((size * rows,) + v.shape[1:], v.dtype)
    out = lax.dynamic_update_slice_in_dim(out, v, at[axis] * rows, 0)
    for by, x in enumerate(got):
        out = lax.dynamic_update_slice_in_dim(out, x, ((at[axis] - by - 1) % size) * rows, 0)
    return out


def after(x, *earlier):
    return lax.optimization_barrier((x,) + earlier)[0]


ORDERS = (
    ("c( d0 d1 c)", "y( y) r0 z(", "b0 b1 z) x(", "r1 x) Z( n0", "Z) Y( n1", "Y) C( C)"),
    ("c( d0 d1 c)", "y( y) r0 z(", "b0 b1 z) x(", "r1 n0 x)", "n1 Z( Z) g0", "Y( g1 Y)", "C( C)"),
)


def settle(own, g_right, g_below, g_corner, probe_now, grad, weight_sum, at, gather):
    def all_turned(pieces, axis):
        return [turned(x, axis, by + 1) for by, x in enumerate(pieces)]

    flat = grad.reshape(2 * W, W)
    tag = jnp.full((8, W), 1.0, F32) * weight_sum
    start, rows = jnp.zeros((), jnp.int32), 2 * W
    corner, below, right, tile, t_right, t_below, t_corner = ([None] * CHUNKS for _ in range(7))
    seen = ()
    for step in " ".join(ORDERS[gather]).split():
        kind, i = step[0], int(step[1:]) if step[1:].isdigit() else None
        wait = lambda x: after(x, *seen) if seen else x
        axis = kind.lower()
        if step in ("c(", "y(", "z("):
            pieces = pieces_of(wait(flat), tag, axis, at)
            got = all_turned(pieces, axis)
            seen = tuple(pieces)
        elif step in ("c)", "y)", "z)"):
            flat, tag = sum_up(flat, tag, [wait(got[0])] + got[1:], axis, at)
            rows //= SIZES[axis]
            start = start + at[axis] * rows
            seen = (flat,)
        elif step == "x(":
            both = jnp.concatenate([wait(flat), tag], 0)
            got = all_turned([both] * 3, axis)
            seen = (both,)
        elif step == "x)":
            both = sum_in_order(both, [wait(got[0])] + got[1:], axis, at)
            leaf = lax.dynamic_slice_in_dim(probe_now.reshape(2 * W, W), start, rows, 0)
            leaf = leaf + both[:rows] / both[rows, 0]
            seen = (leaf,)
        elif step in ("Z(", "Y(", "C("):
            leaf = wait(leaf)
            got = all_turned([leaf] * (SIZES[axis] - 1), axis)
            seen = (leaf,)
        elif step in ("Z)", "Y)", "C)"):
            leaf = placed_in(leaf, [wait(got[0])] + got[1:], axis, at)
            seen = (leaf,)
        elif kind == "d":
            corner[i] = shifted(wait(g_corner[i]), "tr", 1)
        elif kind == "b":
            below[i] = shifted(wait(g_below[i]), "tr", 1)
        elif kind == "r":
            new = g_right[i] + wait(corner[i])
            seen = (new,)
            right[i] = shifted(new, "tc", 1)
        elif kind == "n":
            tile[i] = own[i] + wait(below[i]) + right[i]
            seen = (tile[i],)
            if gather:
                t_right[i] = shifted(tile[i], "tc", -1)
                t_below[i] = shifted(tile[i], "tr", -1)
        elif gather:
            new = wait(t_right[i])
            seen = (new,)
            t_corner[i] = shifted(new, "tr", -1)
    return tile, (t_right, t_below, t_corner), leaf.reshape(2, W, W)


def tables():
    index = lax.optimization_barrier(jnp.arange(Q, dtype=jnp.int32))
    four = 4 * index[None, :, None] + jnp.arange(4, dtype=jnp.int32)[:, None, None]
    angle = (four * index[None, None, :] % W).astype(F32) * (2.0 * math.pi / W)
    c, s = jnp.cos(angle) / math.sqrt(W), jnp.sin(angle) / math.sqrt(W)
    whole = jnp.concatenate([jnp.concatenate([c, s], 2), jnp.concatenate([-s, c], 2)], 1)
    turn = lambda a: jnp.swapaxes(a, 1, 2)
    rounded = lax.reduce_precision(whole, 8, 7)
    high, low = rounded.astype(BF), (whole - rounded).astype(BF)
    return high, low, turn(high), turn(low)


def split(x):
    high = x.astype(BF)
    return high, (x - high.astype(F32)).astype(BF)


def sums(x):
    return x[0] + x[2], x[0] - x[2], x[1] + x[3], x[1] - x[3]


def forward4(re, im):
    s0r, d0r, s1r, d1r = sums(re)
    s0i, d0i, s1i, d1i = sums(im)
    return [
        (s0r + s1r, s0i + s1i),
        (d0r + d1i, d0i - d1r),
        (s0r - s1r, s0i - s1i),
        (d0r - d1i, d0i + d1r),
    ]


def inverse4(re, im):
    s0r, d0r, s1r, d1r = sums(re)
    s0i, d0i, s1i, d1i = sums(im)
    return [
        (s0r + s1r, s0i + s1i),
        (d0r - d1i, d0i + d1r),
        (s0r - s1r, s0i - s1i),
        (d0r + d1i, d0i - d1r),
    ]


def dot(a, b):
    return jnp.dot(a, b, preferred_element_type=F32)


def at_row(start, count):
    return pl.ds(pl.multiple_of(start, 8), count)


def at_row32(start, count):
    return pl.ds(pl.multiple_of(start, 32), count)


def order_kernel(m_ref, o_ref, held):
    row = lax.broadcasted_iota(jnp.int32, (W, W), 0)
    col = lax.broadcasted_iota(jnp.int32, (W, W), 1)
    pick = jnp.where(row == 4 * (col % Q) + col // Q, 1.0, 0.0).astype(BF)
    for v in range(2):
        for b in range(4):
            held[b * W : (b + 1) * W, :] = m_ref[v, :, b * Q : (b + 1) * Q]
        for q in range(4):
            x = jnp.concatenate([held[pl.ds(b * W + q, Q, stride=4), :] for b in range(4)], 1)
            high = x.astype(BF)
            rest = x - high.astype(F32)
            mid, low = split(rest)
            o_ref[v, q * Q : (q + 1) * Q, :] = (dot(high, pick) + dot(mid, pick)) + dot(low, pick)


def ordered(m):
    vm = pl.BlockSpec(memory_space=pltpu.VMEM)
    return pl.pallas_call(
        order_kernel,
        out_shape=jax.ShapeDtypeStruct((2, W, W), F32),
        in_specs=[vm],
        out_specs=vm,
        scratch_shapes=[pltpu.VMEM((4 * W, Q), F32)],
        compiler_params=pltpu.CompilerParams(vmem_limit_bytes=32 * 1024 * 1024),
        cost_estimate=pl.CostEstimate(flops=6 * W**3 * 2, bytes_accessed=16 * W * W, transcendentals=0),
        name="order",
    )(m)


def views_kernel(sc, wt, *refs):
    n = CHUNKS
    t_refs, r_refs, b_refs, d_refs = (refs[k * n : (k + 1) * n] for k in range(4))
    refs = refs[4 * n :]
    p_ref, m_ref, mh, ml, th, tl = refs[:6]
    refs = refs[6:]
    own_refs, gr_refs, gb_refs, gd_refs = (refs[k * n : (k + 1) * n] for k in range(4))
    pg_ref, pr, s1, xx, dd, ee, zz, pp = refs[4 * n :]
    span = W // ROWS

    def roll_rows(t, top):
        rows, rows2 = at_row(t * RB, RB), at_row(t * RB + W, RB)
        before = at_row(jnp.where(t == 0, W - 8, t * RB - 8), 8)
        re, im = p_ref[0, rows, :], p_ref[1, rows, :]
        for k, x in ((0, re), (1, im)):
            x = jnp.concatenate([p_ref[k, before, :], x], 0)
            for v in range(2):
                y = pltpu.roll(pltpu.roll(x, sc[2 * v + 1], 1), sc[2 * v] & 7, 0)[8:]
                pr[v, k, rows, :] = y
                pr[v, k, rows2, :] = y
        return jnp.maximum(top, re * re + im * im)

    top = lax.fori_loop(0, W // RB, roll_rows, jnp.zeros((RB, W), F32))
    step = 1.0 / (jnp.max(top) + EPS)
    lanes = lax.broadcasted_iota(jnp.int32, (1, W), 1)

    def pick(v, chunk, start, count):
        row = chunk * span + start + lax.broadcasted_iota(jnp.int32, (count, 1), 0)
        below = jnp.broadcast_to(row < sc[2 * v], (count, W))
        right = jnp.broadcast_to(lanes < sc[2 * v + 1], (count, W))
        rows = at_row(start, count)
        out = []
        for k in range(2):
            upper = jnp.where(right, r_refs[k * ROWS + chunk][rows, :], t_refs[k * ROWS + chunk][rows, :])
            lower = jnp.where(right, d_refs[k * ROWS + chunk][rows, :], b_refs[k * ROWS + chunk][rows, :])
            out.append(jnp.where(below, lower, upper))
        return out[0], out[1], below, right

    def probe_rows(v, row, count):
        rows = at_row(W - (sc[2 * v] & -8) + row, count)
        return pr[v, 0, rows, :], pr[v, 1, rows, :]

    for v in range(2):

        def first(t, _):
            base = t * RB
            for p in range(4):
                chunk, start = divmod(p * Q, span)
                are, aim, _, _ = pick(v, chunk, start + base, RB)
                pre, pim = probe_rows(v, base + p * Q, RB)
                wr, wi = pre * are - pim * aim, pre * aim + pim * are
                cols = [slice(q * Q, (q + 1) * Q) for q in range(4)]
                o = slice(p * RB, (p + 1) * RB)
                for q, (br, bi) in enumerate(forward4([wr[:, c] for c in cols], [wi[:, c] for c in cols])):
                    s1[q, o, 0:128], s1[q, o, 256:384] = split(br)
                    s1[q, o, 128:256], s1[q, o, 384:512] = split(bi)
            for q in range(4):
                high, low = s1[q, :, 0:256], s1[q, :, 256:512]
                a = dot(high, th[q]) + dot(low, th[q]) + dot(high, tl[q])
                re = [a[p * RB : (p + 1) * RB, 0:Q] for p in range(4)]
                im = [a[p * RB : (p + 1) * RB, Q:] for p in range(4)]
                c = slice(q * Q, (q + 1) * Q)
                for u, (br, bi) in enumerate(forward4(re, im)):
                    xx[u, at_row32(base, RB), c], xx[u, at_row32(base + 256, RB), c] = split(br)
                    xx[u, at_row32(base + 128, RB), c], xx[u, at_row32(base + 384, RB), c] = split(bi)
            return 0

        lax.fori_loop(0, Q // RB, first, 0)
        for half in range(1):
            cs = slice(0, 512)

            def middle(u):
                high, low = xx[u, 0:256, cs], xx[u, 256:512, cs]
                far = dot(mh[u], high) + dot(mh[u], low) + dot(ml[u], high)
                re, im = far[0:Q], far[Q:]
                size = jnp.maximum(re * re + im * im, FLOOR * FLOOR)
                f = m_ref[v, at_row(u * Q, Q), cs] * lax.rsqrt(size) - 1.0
                dd[0:128, :], dd[256:384, :] = split(re * f)
                dd[128:256, :], dd[384:512, :] = split(im * f)
                high, low = dd[0:256, :], dd[256:512, :]
                ee[u] = dot(th[u], high) + dot(th[u], low) + dot(tl[u], high)
                return 0

            [middle(u) for u in range(4)]

            def turn(t, _):
                ro, io = at_row(t * RB, RB), at_row(t * RB + Q, RB)
                for h in range(4):
                    c = slice(h * Q, (h + 1) * Q)
                    qc = 2 * half + h
                    parts = inverse4([ee[u, ro, c] for u in range(4)], [ee[u, io, c] for u in range(4)])
                    for p, (zr, zi) in enumerate(parts):
                        o = at_row32(t * RB + p * Q, RB)
                        zz[v, qc, o, 0:128], zz[v, qc, o, 256:384] = split(zr)
                        zz[v, qc, o, 128:256], zz[v, qc, o, 384:512] = split(zi)
                return 0

            lax.fori_loop(0, Q // RB, turn, 0)

    for chunk in range(ROWS):

        def last(t, _):
            start = t * R4
            rows = at_row(start, R4)
            all_rows = at_row32(chunk * span + start, R4)
            for v in range(2):
                e = []
                for q in range(4):
                    high, low = zz[v, q, all_rows, 0:256], zz[v, q, all_rows, 256:512]
                    e.append(dot(high, mh[q]) + dot(low, mh[q]) + dot(high, ml[q]))
                parts = inverse4([x[:, 0:Q] for x in e], [x[:, Q:] for x in e])
                cr = jnp.concatenate([x[0] for x in parts], 1) * wt[v]
                ci = jnp.concatenate([x[1] for x in parts], 1) * wt[v]
                are, aim, below, right = pick(v, chunk, start, R4)
                pre, pim = probe_rows(v, chunk * span + start, R4)
                grad = ((pre * cr + pim * ci) * step, (pre * ci - pim * cr) * step)
                pp[v, 0, all_rows, :] = pltpu.roll(are * cr + aim * ci, W - sc[2 * v + 1], 1)
                pp[v, 1, all_rows, :] = pltpu.roll(are * ci - aim * cr, W - sc[2 * v + 1], 1)
                none = jnp.zeros_like(cr)
                for k in range(2):
                    upper, lower = jnp.where(below, none, grad[k]), jnp.where(below, grad[k], none)
                    terms = (
                        (own_refs, jnp.where(right, none, upper)),
                        (gr_refs, jnp.where(right, upper, none)),
                        (gb_refs, jnp.where(right, none, lower)),
                        (gd_refs, jnp.where(right, lower, none)),
                    )
                    for which, term in terms:
                        if v == 0:
                            if which is own_refs:
                                term = term + t_refs[k * ROWS + chunk][rows, :]
                            which[k * ROWS + chunk][rows, :] = term
                        else:
                            which[k * ROWS + chunk][rows, :] += term
            return 0

        lax.fori_loop(0, span // R4, last, 0, unroll=2)

    def double(t, _):
        rows, rows2 = at_row(t * RB, RB), at_row(t * RB + W, RB)
        for v in range(2):
            for k in range(2):
                x = pp[v, k, rows, :]
                pr[v, k, rows, :] = x
                pr[v, k, rows2, :] = x
        return 0

    lax.fori_loop(0, W // RB, double, 0)

    def back(t, _):
        for k in range(2):
            total = None
            for v in range(2):
                x = pr[v, k, at_row((sc[2 * v] & -8) + t * RB, RB + 8), :]
                x = pltpu.roll(x, RB + 8 - (sc[2 * v] & 7), 0)[:RB]
                total = x if total is None else total + x
            pg_ref[k, at_row(t * RB, RB), :] = total
        return 0

    lax.fori_loop(0, W // RB, back, 0)


def views(sc, wt, tiles, probe_now, moduli, tabs):
    vm, sm = pl.BlockSpec(memory_space=pltpu.VMEM), pl.BlockSpec(memory_space=pltpu.SMEM)
    part = jax.ShapeDtypeStruct((W // ROWS, W), F32)
    out = pl.pallas_call(
        views_kernel,
        out_shape=(part,) * (4 * CHUNKS) + (jax.ShapeDtypeStruct((2, W, W), F32),),
        in_specs=[sm, sm] + [vm] * (4 * CHUNKS + 6),
        out_specs=(vm,) * (4 * CHUNKS + 1),
        scratch_shapes=[
            pltpu.VMEM((2, 2, 2 * W, W), F32),
            pltpu.VMEM((4, 4 * RB, 512), BF),
            pltpu.VMEM((4, 512, W), BF),
            pltpu.VMEM((512, 512), BF),
            pltpu.VMEM((4, 256, 512), F32),
            pltpu.VMEM((2, 4, W, 512), BF),
            pltpu.VMEM((2, 2, W, W), F32),
        ],
        compiler_params=pltpu.CompilerParams(vmem_limit_bytes=58 * 1024 * 1024),
        cost_estimate=pl.CostEstimate(flops=26 * 10**9, bytes_accessed=28 * 2**20, transcendentals=2**19),
        name="views",
    )(sc, wt, *[x for tile in tiles for x in tile], probe_now, moduli, *tabs)
    return [out[k * CHUNKS : (k + 1) * CHUNKS] for k in range(4)], out[-1]


def on_device(object_init, probe_init, moduli, corners, live):
    tr, tc = lax.axis_index("tr"), lax.axis_index("tc")
    at = {"x": tc % 4, "y": tc // 4, "z": tr // 2, "c": tr % 2}
    sc = (corners - jnp.stack([tr * W, tc * W])).astype(jnp.int32).reshape(-1)
    wt = live.astype(F32)
    tabs = tables()
    span = W // ROWS
    tile = [object_init[k, i * span : (i + 1) * span] for k in range(2) for i in range(ROWS)]
    probe_now = probe_init
    measured = ordered(moduli)
    t_right = [shifted(x, "tc", -1) for x in tile]
    t_below = [shifted(x, "tr", -1) for x in tile]
    t_corner = [shifted(x, "tr", -1) for x in t_right]
    around = (t_right, t_below, t_corner)
    for iteration in range(ITERS):
        (own, g_right, g_below, g_corner), grad = views(
            sc, wt, (tile,) + around, probe_now, measured, tabs
        )
        tile, around, probe_now = settle(
            own, g_right, g_below, g_corner, probe_now, grad, jnp.sum(wt), at, iteration + 1 < ITERS
        )
    return jnp.concatenate(tile, 0).reshape(2, W, W), probe_now


def solution(mesh):
    placed = (
        P(None, "tr", "tc"),
        P(),
        P(("tr", "tc"), None, None),
        P(("tr", "tc"), None),
        P(("tr", "tc")),
    )
    return jax.shard_map(
        on_device, mesh=mesh, in_specs=placed, out_specs=(P(None, "tr", "tc"), P()), check_vma=False
    )
```

```python
import math

import jax
import jax.numpy as jnp
from jax import lax
from jax.experimental import pallas as pl
from jax.experimental.pallas import tpu as pltpu
from jax.sharding import PartitionSpec as P


ITERS = 2
W = 512
Q = 128
ROWS = 1
CHUNKS = 2 * ROWS
FLOOR = 0.1
EPS = 1e-06
F32 = jnp.float32
BF = jnp.bfloat16
RB = 32
R4 = 128
AXES = ("tr", "tc")
SIZES = {"c": 2, "x": 4, "y": 4, "z": 4}


def shifted(x, axis, by):
    peers = lax.axis_size(axis)
    pairs = [(i, i + by) for i in range(peers) if 0 <= i + by < peers]
    return lax.ppermute(x, axis, pairs)


def turned(x, axis, by):
    pairs = []
    for tr in range(8):
        for tc in range(16):
            at = {"x": tc % 4, "y": tc // 4, "z": tr // 2, "c": tr % 2}
            to = dict(at)
            to[axis] = (at[axis] + by) % SIZES[axis]
            pairs.append((tr * 16 + tc, (to["z"] * 2 + to["c"]) * 16 + to["y"] * 4 + to["x"]))
    return lax.ppermute(x, AXES, pairs)


def pieces_of(v, tag, axis, at):
    size = SIZES[axis]
    rows = v.shape[0] // size
    out = []
    for by in range(1, size):
        piece = lax.dynamic_slice_in_dim(v, ((at[axis] + by) % size) * rows, rows, 0)
        out.append(jnp.concatenate([piece, tag], 0))
    return out


def sum_up(v, tag, got, axis, at):
    rows = v.shape[0] // SIZES[axis]
    whole = lax.dynamic_slice_in_dim(v, at[axis] * rows, rows, 0)
    for x in got:
        whole, tag = whole + x[:rows], tag + x[rows:]
    return whole, tag


def sum_in_order(own, got, axis, at):
    size = SIZES[axis]
    got = [own] + got
    whole = None
    for k in range(size):
        term = got[0]
        for by in range(1, size):
            term = jnp.where((at[axis] - by) % size == k, got[by], term)
        whole = term if whole is None else whole + term
    return whole


def placed_in(v, got, axis, at):
    size, rows = SIZES[axis], v.shape[0]
    out = jnp.zeros((size * rows,) + v.shape[1:], v.dtype)
    out = lax.dynamic_update_slice_in_dim(out, v, at[axis] * rows, 0)
    for by, x in enumerate(got):
        out = lax.dynamic_update_slice_in_dim(out, x, ((at[axis] - by - 1) % size) * rows, 0)
    return out


def after(x, *earlier):
    return lax.optimization_barrier((x,) + earlier)[0]


ORDERS = (
    ("c( d0 d1 c)", "y( y) r0 z(", "b0 b1 z) x(", "r1 x) Z( n0", "Z) Y( n1", "Y) C( C)"),
    ("c( d0 d1 c)", "y( y) r0 z(", "b0 b1 z) x(", "r1 n0 x)", "n1 Z( Z) g0", "Y( g1 Y)", "C( C)"),
)


def settle(own, g_right, g_below, g_corner, probe_now, grad, weight_sum, at, gather):
    def all_turned(pieces, axis):
        return [turned(x, axis, by + 1) for by, x in enumerate(pieces)]

    flat = grad.reshape(2 * W, W)
    tag = jnp.full((8, W), 1.0, F32) * weight_sum
    start, rows = jnp.zeros((), jnp.int32), 2 * W
    corner, below, right, tile, t_right, t_below, t_corner = ([None] * CHUNKS for _ in range(7))
    seen = ()
    for step in " ".join(ORDERS[gather]).split():
        kind, i = step[0], int(step[1:]) if step[1:].isdigit() else None
        wait = lambda x: after(x, *seen) if seen else x
        axis = kind.lower()
        if step in ("c(", "y(", "z("):
            pieces = pieces_of(wait(flat), tag, axis, at)
            got = all_turned(pieces, axis)
            seen = tuple(pieces)
        elif step in ("c)", "y)", "z)"):
            flat, tag = sum_up(flat, tag, [wait(got[0])] + got[1:], axis, at)
            rows //= SIZES[axis]
            start = start + at[axis] * rows
            seen = (flat,)
        elif step == "x(":
            both = jnp.concatenate([wait(flat), tag], 0)
            got = all_turned([both] * 3, axis)
            seen = (both,)
        elif step == "x)":
            both = sum_in_order(both, [wait(got[0])] + got[1:], axis, at)
            leaf = lax.dynamic_slice_in_dim(probe_now.reshape(2 * W, W), start, rows, 0)
            leaf = leaf + both[:rows] / both[rows, 0]
            seen = (leaf,)
        elif step in ("Z(", "Y(", "C("):
            leaf = wait(leaf)
            got = all_turned([leaf] * (SIZES[axis] - 1), axis)
            seen = (leaf,)
        elif step in ("Z)", "Y)", "C)"):
            leaf = placed_in(leaf, [wait(got[0])] + got[1:], axis, at)
            seen = (leaf,)
        elif kind == "d":
            corner[i] = shifted(wait(g_corner[i]), "tr", 1)
        elif kind == "b":
            below[i] = shifted(wait(g_below[i]), "tr", 1)
        elif kind == "r":
            new = g_right[i] + wait(corner[i])
            seen = (new,)
            right[i] = shifted(new, "tc", 1)
        elif kind == "n":
            tile[i] = own[i] + wait(below[i]) + right[i]
            seen = (tile[i],)
            if gather:
                t_right[i] = shifted(tile[i], "tc", -1)
                t_below[i] = shifted(tile[i], "tr", -1)
        elif gather:
            new = wait(t_right[i])
            seen = (new,)
            t_corner[i] = shifted(new, "tr", -1)
    return tile, (t_right, t_below, t_corner), leaf.reshape(2, W, W)


def tables():
    index = lax.optimization_barrier(jnp.arange(Q, dtype=jnp.int32))
    four = 4 * index[None, :, None] + jnp.arange(4, dtype=jnp.int32)[:, None, None]
    angle = (four * index[None, None, :] % W).astype(F32) * (2.0 * math.pi / W)
    c, s = jnp.cos(angle) / math.sqrt(W), jnp.sin(angle) / math.sqrt(W)
    whole = jnp.concatenate([jnp.concatenate([c, s], 2), jnp.concatenate([-s, c], 2)], 1)
    turn = lambda a: jnp.swapaxes(a, 1, 2)
    rounded = lax.reduce_precision(whole, 8, 7)
    high, low = rounded.astype(BF), (whole - rounded).astype(BF)
    return high, low, turn(high), turn(low)


def split(x):
    high = x.astype(BF)
    return high, (x - high.astype(F32)).astype(BF)


def sums(x):
    return x[0] + x[2], x[0] - x[2], x[1] + x[3], x[1] - x[3]


def forward4(re, im):
    s0r, d0r, s1r, d1r = sums(re)
    s0i, d0i, s1i, d1i = sums(im)
    return [
        (s0r + s1r, s0i + s1i),
        (d0r + d1i, d0i - d1r),
        (s0r - s1r, s0i - s1i),
        (d0r - d1i, d0i + d1r),
    ]


def inverse4(re, im):
    s0r, d0r, s1r, d1r = sums(re)
    s0i, d0i, s1i, d1i = sums(im)
    return [
        (s0r + s1r, s0i + s1i),
        (d0r - d1i, d0i + d1r),
        (s0r - s1r, s0i - s1i),
        (d0r + d1i, d0i - d1r),
    ]


def dot(a, b):
    return jnp.dot(a, b, preferred_element_type=F32)


def at_row(start, count):
    return pl.ds(pl.multiple_of(start, 8), count)


def at_row32(start, count):
    return pl.ds(pl.multiple_of(start, 32), count)


def order_kernel(m_ref, o_ref, held):
    row = lax.broadcasted_iota(jnp.int32, (W, W), 0)
    col = lax.broadcasted_iota(jnp.int32, (W, W), 1)
    pick = jnp.where(row == 4 * (col % Q) + col // Q, 1.0, 0.0).astype(BF)
    for v in range(2):
        for b in range(4):
            held[b * W : (b + 1) * W, :] = m_ref[v, :, b * Q : (b + 1) * Q]
        for q in range(4):
            x = jnp.concatenate([held[pl.ds(b * W + q, Q, stride=4), :] for b in range(4)], 1)
            high = x.astype(BF)
            rest = x - high.astype(F32)
            mid, low = split(rest)
            o_ref[v, q * Q : (q + 1) * Q, :] = (dot(high, pick) + dot(mid, pick)) + dot(low, pick)


def ordered(m):
    vm = pl.BlockSpec(memory_space=pltpu.VMEM)
    return pl.pallas_call(
        order_kernel,
        out_shape=jax.ShapeDtypeStruct((2, W, W), F32),
        in_specs=[vm],
        out_specs=vm,
        scratch_shapes=[pltpu.VMEM((4 * W, Q), F32)],
        compiler_params=pltpu.CompilerParams(vmem_limit_bytes=32 * 1024 * 1024),
        cost_estimate=pl.CostEstimate(flops=6 * W**3 * 2, bytes_accessed=16 * W * W, transcendentals=0),
        name="order",
    )(m)


def views_kernel(sc, wt, *refs):
    n = CHUNKS
    t_refs, r_refs, b_refs, d_refs = (refs[k * n : (k + 1) * n] for k in range(4))
    refs = refs[4 * n :]
    p_ref, m_ref, mh, ml, th, tl = refs[:6]
    refs = refs[6:]
    own_refs, gr_refs, gb_refs, gd_refs = (refs[k * n : (k + 1) * n] for k in range(4))
    pg_ref, pr, s1, xx, dd, ee, zz, pp = refs[4 * n :]
    span = W // ROWS

    def roll_rows(t, top):
        rows, rows2 = at_row(t * RB, RB), at_row(t * RB + W, RB)
        before = at_row(jnp.where(t == 0, W - 8, t * RB - 8), 8)
        re, im = p_ref[0, rows, :], p_ref[1, rows, :]
        for k, x in ((0, re), (1, im)):
            x = jnp.concatenate([p_ref[k, before, :], x], 0)
            for v in range(2):
                y = pltpu.roll(pltpu.roll(x, sc[2 * v + 1], 1), sc[2 * v] & 7, 0)[8:]
                pr[v, k, rows, :] = y
                pr[v, k, rows2, :] = y
        return jnp.maximum(top, re * re + im * im)

    top = lax.fori_loop(0, W // RB, roll_rows, jnp.zeros((RB, W), F32))
    step = 1.0 / (jnp.max(top) + EPS)
    lanes = lax.broadcasted_iota(jnp.int32, (1, W), 1)

    def pick(v, chunk, start, count):
        row = chunk * span + start + lax.broadcasted_iota(jnp.int32, (count, 1), 0)
        below = jnp.broadcast_to(row < sc[2 * v], (count, W))
        right = jnp.broadcast_to(lanes < sc[2 * v + 1], (count, W))
        rows = at_row(start, count)
        out = []
        for k in range(2):
            upper = jnp.where(right, r_refs[k * ROWS + chunk][rows, :], t_refs[k * ROWS + chunk][rows, :])
            lower = jnp.where(right, d_refs[k * ROWS + chunk][rows, :], b_refs[k * ROWS + chunk][rows, :])
            out.append(jnp.where(below, lower, upper))
        return out[0], out[1], below, right

    def probe_rows(v, row, count):
        rows = at_row(W - (sc[2 * v] & -8) + row, count)
        return pr[v, 0, rows, :], pr[v, 1, rows, :]

    def one_view(v, _):

        def first(t, _):
            base = t * RB
            for p in range(4):
                chunk, start = divmod(p * Q, span)
                are, aim, _, _ = pick(v, chunk, start + base, RB)
                pre, pim = probe_rows(v, base + p * Q, RB)
                wr, wi = pre * are - pim * aim, pre * aim + pim * are
                cols = [slice(q * Q, (q + 1) * Q) for q in range(4)]
                o = slice(p * RB, (p + 1) * RB)
                for q, (br, bi) in enumerate(forward4([wr[:, c] for c in cols], [wi[:, c] for c in cols])):
                    s1[q, o, 0:128], s1[q, o, 256:384] = split(br)
                    s1[q, o, 128:256], s1[q, o, 384:512] = split(bi)
            for q in range(4):
                high, low = s1[q, :, 0:256], s1[q, :, 256:512]
                a = dot(high, th[q]) + dot(low, th[q]) + dot(high, tl[q])
                re = [a[p * RB : (p + 1) * RB, 0:Q] for p in range(4)]
                im = [a[p * RB : (p + 1) * RB, Q:] for p in range(4)]
                c = slice(q * Q, (q + 1) * Q)
                for u, (br, bi) in enumerate(forward4(re, im)):
                    xx[u, at_row32(base, RB), c], xx[u, at_row32(base + 256, RB), c] = split(br)
                    xx[u, at_row32(base + 128, RB), c], xx[u, at_row32(base + 384, RB), c] = split(bi)
            return 0

        lax.fori_loop(0, Q // RB, first, 0)
        for half in range(1):
            cs = slice(0, 512)

            def middle(u, _):
                high, low = xx[u, 0:256, cs], xx[u, 256:512, cs]
                far = dot(mh[u], high) + dot(mh[u], low) + dot(ml[u], high)
                re, im = far[0:Q], far[Q:]
                size = jnp.maximum(re * re + im * im, FLOOR * FLOOR)
                f = m_ref[v, at_row(u * Q, Q), cs] * lax.rsqrt(size) - 1.0
                dd[0:128, :], dd[256:384, :] = split(re * f)
                dd[128:256, :], dd[384:512, :] = split(im * f)
                high, low = dd[0:256, :], dd[256:512, :]
                ee[u] = dot(th[u], high) + dot(th[u], low) + dot(tl[u], high)
                return 0

            lax.fori_loop(0, 4, middle, 0, unroll=2)

            def turn(t, _):
                ro, io = at_row(t * RB, RB), at_row(t * RB + Q, RB)
                for h in range(4):
                    c = slice(h * Q, (h + 1) * Q)
                    qc = 2 * half + h
                    parts = inverse4([ee[u, ro, c] for u in range(4)], [ee[u, io, c] for u in range(4)])
                    for p, (zr, zi) in enumerate(parts):
                        o = at_row32(t * RB + p * Q, RB)
                        zz[v, qc, o, 0:128], zz[v, qc, o, 256:384] = split(zr)
                        zz[v, qc, o, 128:256], zz[v, qc, o, 384:512] = split(zi)
                return 0

            lax.fori_loop(0, Q // RB, turn, 0)

        return 0

    lax.fori_loop(0, 2, one_view, 0)

    for chunk in range(ROWS):

        def last(t, _):
            start = t * R4
            rows = at_row(start, R4)
            all_rows = at_row32(chunk * span + start, R4)
            for v in range(2):
                e = []
                for q in range(4):
                    high, low = zz[v, q, all_rows, 0:256], zz[v, q, all_rows, 256:512]
                    e.append(dot(high, mh[q]) + dot(low, mh[q]) + dot(high, ml[q]))
                parts = inverse4([x[:, 0:Q] for x in e], [x[:, Q:] for x in e])
                cr = jnp.concatenate([x[0] for x in parts], 1) * wt[v]
                ci = jnp.concatenate([x[1] for x in parts], 1) * wt[v]
                are, aim, below, right = pick(v, chunk, start, R4)
                pre, pim = probe_rows(v, chunk * span + start, R4)
                grad = ((pre * cr + pim * ci) * step, (pre * ci - pim * cr) * step)
                pp[v, 0, all_rows, :] = pltpu.roll(are * cr + aim * ci, W - sc[2 * v + 1], 1)
                pp[v, 1, all_rows, :] = pltpu.roll(are * ci - aim * cr, W - sc[2 * v + 1], 1)
                none = jnp.zeros_like(cr)
                for k in range(2):
                    upper, lower = jnp.where(below, none, grad[k]), jnp.where(below, grad[k], none)
                    terms = (
                        (own_refs, jnp.where(right, none, upper)),
                        (gr_refs, jnp.where(right, upper, none)),
                        (gb_refs, jnp.where(right, none, lower)),
                        (gd_refs, jnp.where(right, lower, none)),
                    )
                    for which, term in terms:
                        if v == 0:
                            if which is own_refs:
                                term = term + t_refs[k * ROWS + chunk][rows, :]
                            which[k * ROWS + chunk][rows, :] = term
                        else:
                            which[k * ROWS + chunk][rows, :] += term
            return 0

        lax.fori_loop(0, span // R4, last, 0)

    def double(t, _):
        rows, rows2 = at_row(t * RB, RB), at_row(t * RB + W, RB)
        for v in range(2):
            for k in range(2):
                x = pp[v, k, rows, :]
                pr[v, k, rows, :] = x
                pr[v, k, rows2, :] = x
        return 0

    lax.fori_loop(0, W // RB, double, 0)

    def back(t, _):
        for k in range(2):
            total = None
            for v in range(2):
                x = pr[v, k, at_row((sc[2 * v] & -8) + t * RB, RB + 8), :]
                x = pltpu.roll(x, RB + 8 - (sc[2 * v] & 7), 0)[:RB]
                total = x if total is None else total + x
            pg_ref[k, at_row(t * RB, RB), :] = total
        return 0

    lax.fori_loop(0, W // RB, back, 0)


def views(sc, wt, tiles, probe_now, moduli, tabs):
    vm, sm = pl.BlockSpec(memory_space=pltpu.VMEM), pl.BlockSpec(memory_space=pltpu.SMEM)
    part = jax.ShapeDtypeStruct((W // ROWS, W), F32)
    out = pl.pallas_call(
        views_kernel,
        out_shape=(part,) * (4 * CHUNKS) + (jax.ShapeDtypeStruct((2, W, W), F32),),
        in_specs=[sm, sm] + [vm] * (4 * CHUNKS + 6),
        out_specs=(vm,) * (4 * CHUNKS + 1),
        scratch_shapes=[
            pltpu.VMEM((2, 2, 2 * W, W), F32),
            pltpu.VMEM((4, 4 * RB, 512), BF),
            pltpu.VMEM((4, 512, W), BF),
            pltpu.VMEM((512, 512), BF),
            pltpu.VMEM((4, 256, 512), F32),
            pltpu.VMEM((2, 4, W, 512), BF),
            pltpu.VMEM((2, 2, W, W), F32),
        ],
        compiler_params=pltpu.CompilerParams(vmem_limit_bytes=58 * 1024 * 1024),
        cost_estimate=pl.CostEstimate(flops=26 * 10**9, bytes_accessed=28 * 2**20, transcendentals=2**19),
        name="views",
    )(sc, wt, *[x for tile in tiles for x in tile], probe_now, moduli, *tabs)
    return [out[k * CHUNKS : (k + 1) * CHUNKS] for k in range(4)], out[-1]


def on_device(object_init, probe_init, moduli, corners, live):
    tr, tc = lax.axis_index("tr"), lax.axis_index("tc")
    at = {"x": tc % 4, "y": tc // 4, "z": tr // 2, "c": tr % 2}
    sc = (corners - jnp.stack([tr * W, tc * W])).astype(jnp.int32).reshape(-1)
    wt = live.astype(F32)
    tabs = tables()
    span = W // ROWS
    planes = (object_init[0], lax.optimization_barrier(object_init)[1])
    tile = [x[i * span : (i + 1) * span] for x in planes for i in range(ROWS)]
    probe_now = probe_init
    measured = ordered(moduli)
    t_right = [shifted(x, "tc", -1) for x in tile]
    t_below = [shifted(x, "tr", -1) for x in tile]
    t_corner = [shifted(x, "tr", -1) for x in t_right]
    around = (t_right, t_below, t_corner)
    for iteration in range(ITERS):
        (own, g_right, g_below, g_corner), grad = views(
            sc, wt, (tile,) + around, probe_now, measured, tabs
        )
        tile, around, probe_now = settle(
            own, g_right, g_below, g_corner, probe_now, grad, jnp.sum(wt), at, iteration + 1 < ITERS
        )
    return jnp.concatenate(tile, 0).reshape(2, W, W), probe_now


def solution(mesh):
    placed = (
        P(None, "tr", "tc"),
        P(),
        P(("tr", "tc"), None, None),
        P(("tr", "tc"), None),
        P(("tr", "tc")),
    )
    return jax.shard_map(
        on_device, mesh=mesh, in_specs=placed, out_specs=(P(None, "tr", "tc"), P()), check_vma=False
    )
```
